32 devices in a mesh: replica: 2 (over y), tensor: 16 (over z, x, core).
Axes of the slice: x: 2, y: 2, z: 4, core: 2. Of those that a mesh axis runs over, the one named last changes fastest.
Arguments:
- tokens: bfloat16 [256, 2560], P('replica', 'tensor'), may hold values from -6 to 6
- next_tokens: bfloat16 [128, 2560], P('replica', 'tensor'), may hold values from -6 to 6
- cotangent: bfloat16 [256, 2560], P('replica', 'tensor'), may hold values from -0.5 to 0.5
- gate_weight: bfloat16 [2560, 14336], P(None, 'tensor'), may hold values from -0.125 to 0.125
- up_weight: bfloat16 [2560, 14336], P(None, 'tensor'), may hold values from -0.125 to 0.125
- down_weight: bfloat16 [14336, 2560], P('tensor'), may hold values from -0.046875 to 0.046875
- momentum: bfloat16 [2, 14336, 2560], P('replica', 'tensor'), may hold values from -6 to 6
- indices: int32 [2, 224, 40, 32], P(None, 'tensor'), may hold values from 0 to 4095, as said below
Outputs:
- output: bfloat16 [128, 2560], P(('replica', 'tensor'))
- new_momentum: bfloat16 [2, 14336, 2560], P('replica', 'tensor')
The draws below stay inside these ranges and needn't reach their ends.
Inputs may be any that keep to these rules, and one draw needn't show every extreme that they name: Within one replica and tile the 32 indices are distinct; the n-th lies in the range from n * 64 * 2 to (n + 1) * 64 * 2 - 1.
All inputs are finite; a program needn't handle non-finite values.
Results may differ from the reference program's by a relative error of at most 0.017.
Values may be sent and summed in bfloat16 or wider, within the bound.
A program may use at most 128 MiB of HBM per device.

```python
import jax
import jax.numpy as jnp
from jax import lax

D = 2560
FF = 14336
TILE = 64
KEEP = 32
TOK = 128
REPLICAS = 2
TOKENS = 256
NEXTS = 128


def draw_indices(key, part):
    stride = TILE * TILE // KEEP
    shape = (REPLICAS, FF // TILE, D // TILE, KEEP)
    offsets = jax.random.randint(key, shape, 0, stride, dtype=jnp.int32)
    base = jnp.arange(KEEP, dtype=jnp.int32) * stride
    return (offsets + base).astype(jnp.int32)


def levels(rng, extent, split, smallest, largest):
    def one(position, blocks):
        steps = jax.random.uniform(jax.random.fold_in(jax.random.fold_in(rng, 6), position), (blocks,), jnp.float32, smallest / len(split), largest / len(split))
        return jnp.repeat(jnp.exp(steps), extent[position] // blocks).reshape((-1,) + (1,) * (len(extent) - position - 1))

    factor_of = one(*split[0])
    for cut in split[1:]:
        factor_of = factor_of * one(*cut)
    return factor_of


def scatter_about(rng, shape, width, bound, cuts=(), kind=jnp.bfloat16):
    entries = width * jax.random.normal(rng, shape, jnp.float32)
    if cuts:
        entries = entries * levels(rng, shape, cuts, -0.22, 0.18)
    return jnp.clip(entries, -bound, bound).astype(kind)


def setup_inputs(seed: int = 0) -> dict:
    key_list = jax.random.split(jax.random.key(seed), 9)
    return {
        "tokens": scatter_about(key_list[0], (TOKENS, D), 1.0, 6.0, ((0, 2), (1, 16))),
        "next_tokens": scatter_about(key_list[1], (NEXTS, D), 1.0, 6.0, ((0, 2), (1, 16))),
        "cotangent": scatter_about(key_list[2], (TOKENS, D), 0.07, 0.5, ((0, 2), (1, 16))),
        "gate_weight": scatter_about(key_list[3], (D, FF), D ** -0.5, 0.125, ((1, 16),)),
        "up_weight": scatter_about(key_list[4], (D, FF), D ** -0.5, 0.125, ((1, 16),)),
        "down_weight": scatter_about(key_list[5], (FF, D), FF ** -0.5, 0.046875, ((0, 16),)),
        "momentum": scatter_about(key_list[6], (REPLICAS, FF, D), 1.0, 6.0, ((0, 2), (1, 16))),
        "indices": draw_indices(jax.random.fold_in(key_list[8], 71), 0),
    }


BETA_DECAY = 0.9
STEP_RATE = 0.1

def cosine_table():
    freq = jnp.arange(TILE, dtype=jnp.float32)[:, None]
    place = jnp.arange(TILE, dtype=jnp.float32)[None, :]
    table = jnp.cos(jnp.pi * (2.0 * place + 1.0) * freq / (2.0 * TILE))
    factor = jnp.where(freq == 0.0, jnp.sqrt(1.0 / TILE), jnp.sqrt(2.0 / TILE))
    return (table * factor).astype(jnp.float32)

def forward_tiles(field, table):
    height, breadth = field.shape
    blocks = field.reshape(height // TILE, TILE, breadth // TILE, TILE)
    spectrum = jnp.einsum('ak,xkyl,bl->xyab', table, blocks, table, precision=lax.Precision.HIGHEST)
    return spectrum.reshape(height // TILE, breadth // TILE, TILE * TILE)

def inverse_tiles(spectrum, table):
    tile_rows, tile_cols, _ = spectrum.shape
    blocks = spectrum.reshape(tile_rows, tile_cols, TILE, TILE)
    field = jnp.einsum('ak,xyab,bl->xkyl', table, blocks, table, precision=lax.Precision.HIGHEST)
    return field.reshape(tile_rows * TILE, tile_cols * TILE)

def place_values(values, where):
    tile_rows, tile_cols, _ = where.shape
    dense = jnp.zeros((tile_rows, tile_cols, TILE * TILE), jnp.float32)
    row_ids = jnp.arange(tile_rows, dtype=jnp.int32)[:, None, None]
    col_ids = jnp.arange(tile_cols, dtype=jnp.int32)[None, :, None]
    return dense.at[row_ids, col_ids, where].add(values)

def swiglu(inputs, gate_weight, up_weight):
    gate = jnp.dot(inputs, gate_weight, preferred_element_type=jnp.float32)
    upper = jnp.dot(inputs, up_weight, preferred_element_type=jnp.float32)
    return (jax.nn.silu(gate) * upper).astype(jnp.bfloat16)

def reference(tokens, next_tokens, cotangent, gate_weight, up_weight, down_weight, momentum, indices):
    table = cosine_table()

    def one_replica(replica):
        start = replica * TOK
        inputs = lax.dynamic_slice_in_dim(tokens, start, TOK, 0)
        grads_out = lax.dynamic_slice_in_dim(cotangent, start, TOK, 0)
        hidden = swiglu(inputs, gate_weight, up_weight)
        grad = jnp.dot(hidden.T, grads_out, preferred_element_type=jnp.float32)
        moment = BETA_DECAY * momentum[replica].astype(jnp.float32) + grad
        spectrum = forward_tiles(moment, table)
        where = indices[replica]
        sent = jnp.take_along_axis(spectrum, where, axis=2).astype(jnp.bfloat16)
        own = place_values(sent.astype(jnp.float32), where)
        kept = (moment - inverse_tiles(own, table)).astype(jnp.bfloat16)
        return (sent, kept)
    sent_all, new_momentum = lax.map(one_replica, jnp.arange(REPLICAS, dtype=jnp.int32))
    where_all = jnp.moveaxis(indices, 0, 2).reshape(FF // TILE, D // TILE, REPLICAS * KEEP)
    values_all = jnp.moveaxis(sent_all.astype(jnp.float32), 0, 2).reshape(FF // TILE, D // TILE, REPLICAS * KEEP)
    total = place_values(values_all, where_all)
    update = inverse_tiles(total, table) / REPLICAS
    new_down = (down_weight.astype(jnp.float32) - STEP_RATE * update).astype(jnp.bfloat16)
    next_hidden = swiglu(next_tokens, gate_weight, up_weight)
    output = jnp.dot(next_hidden, new_down, preferred_element_type=jnp.float32).astype(jnp.bfloat16)
    return (output, new_momentum)
```

```python
import functools

import jax
import jax.numpy as jnp
import numpy as np
from jax import lax
from jax.experimental import pallas as pl
from jax.experimental.pallas import tpu as pltpu
from jax.sharding import PartitionSpec as P

TILE = 64
BETA_DECAY = 0.9
STEP_RATE = 0.1
MESH = pl.DeviceIdType.MESH
ANY = pl.BlockSpec(memory_space=pl.ANY)
VMEM = pl.BlockSpec(memory_space=pltpu.VMEM)
KIND = jnp.bfloat16


def cosine_table():
    freq = np.arange(TILE)[:, None]
    place = np.arange(TILE)[None, :]
    table = np.cos(np.pi * (2.0 * place + 1.0) * freq / (2.0 * TILE))
    return table * np.where(freq == 0, np.sqrt(1.0 / TILE), np.sqrt(2.0 / TILE))


def split_bf16(table):
    high = jnp.asarray(table, jnp.float32).astype(KIND)
    rest = jnp.asarray(table, jnp.float32) - high.astype(jnp.float32)
    return high, rest.astype(KIND)


def halves(count):
    table = cosine_table()
    eye = np.eye(count)
    return np.concatenate([np.kron(eye, table[0::2]), np.kron(eye, table[1::2])], axis=0)


def flip(index, bits):
    bit = 1
    while bit <= bits:
        if bits & bit:
            index = index + bit - 2 * bit * ((index // bit) % 2)
        bit *= 2
    return index


def dot(a, b):
    return jnp.dot(a, b, preferred_element_type=jnp.float32)


def contract(a, b, dim):
    return lax.dot_general(
        a, b, (((dim,), (dim,)), ((), ())), preferred_element_type=jnp.float32
    )


def strip_offsets(indices, which):
    tiles, keep, columns = indices.shape[1:]
    first = lax.broadcasted_iota(jnp.int32, (keep, columns), 0) * (TILE * TILE // keep)
    listed = [
        (indices[which, n] - first).astype(jnp.float32).astype(KIND) for n in range(tiles)
    ]
    return jnp.concatenate(listed, axis=0)


def step_kernel(
    size, replicas, strip, chunk, wide,
    tok, nxt, cot, gate_hbm, upper_hbm, down_hbm, momentum_hbm, indices_hbm,
    row_hbm, turn_hbm, across_hbm, order_hbm,
    out, hidden, grads, pair, momentum,
    nxt_in, held_tok, held_nxt, held_cot,
    gate, upper, down, indices, spread, gather, row, turn, across, order,
    features, basis, early, mine, theirs, total,
    stage_core, held_core, stage_side, held_side, stage_deep, held_deep, split_sum,
    send, recv, local, pass_send, pass_recv, fold_send, fold_recv, deep_send, deep_recv,
):
    depth = size // 4
    me = lax.axis_index("tensor")
    replica = lax.axis_index("replica")
    z, x, core = me // 4, (me // 2) % 2, me % 2
    share, count = tok.shape
    nexts = nxt.shape[0]
    rows, breadth = down.shape
    half = rows // 2
    split = share // 2
    group = 4 * share
    blocks, kept = (tok, held_nxt.at[me], cot), (held_tok, held_nxt, held_cot)

    def slot(zz, xx, cc):
        return (zz * 2 + xx) * 2 + cc

    names = [
        (nxt, nxt_in), (order_hbm, order), (indices_hbm, indices), (across_hbm, across),
        (tok, held_tok.at[me]), (gate_hbm, gate), (upper_hbm, upper), (row_hbm, row),
        (turn_hbm, turn), (momentum_hbm.at[0], momentum), (cot, held_cot.at[me]), (down_hbm, down),
    ]
    loads = [
        pltpu.make_async_copy(source, target, local.at[n])
        for n, (source, target) in enumerate(names)
    ]
    for load in loads:
        load.start()

    others = [flip(z, k) for k in range(1, depth)]
    deep = [slot(zz, x, core) for zz in others]
    side, twin = slot(z, 1 - x, core), slot(z, x, 1 - core)
    barrier = pltpu.get_barrier_semaphore()
    for target in deep + [side, twin]:
        pl.semaphore_signal(barrier, inc=1, device_id={"tensor": target}, device_id_type=MESH)
    for k in range(1, replicas):
        pl.semaphore_signal(
            barrier, inc=1, device_id={"replica": (replica + k) % replicas}, device_id_type=MESH
        )
    ribbon = spread.shape
    spread[...] = jnp.where(
        lax.broadcasted_iota(jnp.int32, ribbon, 1) // TILE
        == lax.broadcasted_iota(jnp.int32, ribbon, 0),
        1.0,
        0.0,
    ).astype(KIND)
    gather[...] = spread[...].T
    pl.semaphore_wait(barrier, depth + replicas)

    copies = []

    def push(kind, which, target, source=None):
        copy = pltpu.make_async_remote_copy(
            src_ref=kept[kind].at[which] if source is None else source,
            dst_ref=kept[kind].at[which],
            send_sem=send.at[len(copies)],
            recv_sem=recv.at[kind, which],
            device_id={"tensor": target},
            device_id_type=MESH,
        )
        copy.start()
        copies.append(copy)

    def arrive(kind, which):
        pltpu.make_async_remote_copy(
            src_ref=blocks[kind],
            dst_ref=kept[kind].at[which],
            send_sem=send.at[0],
            recv_sem=recv.at[kind, which],
            device_id={"tensor": twin},
            device_id_type=MESH,
        ).wait_recv()

    for target in [side] + deep + [twin]:
        push(0, me, target, tok)
    loads[0].wait()
    loads[1].wait()
    turned = contract(nxt_in[...], order[...], 0)
    held_nxt[me] = jnp.concatenate([turned[:split], turned[split:]], axis=1).astype(KIND)
    for target in [side] + deep + [twin]:
        push(1, me, target)
    for target in [side] + deep + [twin]:
        push(2, me, target, cot)

    place = (lax.broadcasted_iota(jnp.int32, (half, chunk), 1) % TILE).astype(jnp.float32)

    def build(slab, which):
        offsets = strip_offsets(indices, which)
        columns = offsets.shape[1]
        for start in range(0, breadth, chunk):
            span = slice(start, start + chunk)
            where = dot(offsets, spread[:columns, span])
            odd = where >= TILE
            hot = jnp.where(jnp.where(odd, where - TILE, where) == place, 1.0, 0.0)
            waves = dot(hot.astype(KIND), across[...])
            basis[slab, :half, span] = jnp.where(odd, 0.0, waves).astype(KIND)
            basis[slab, half:, span] = jnp.where(odd, waves, 0.0).astype(KIND)

    def relay_deep(kinds):
        for kind in kinds:
            for which in deep:
                arrive(kind, which)
                push(kind, which, side)
                push(kind, which, twin)

    def relay_side(kinds):
        for kind in kinds:
            for zz in [z] + others:
                which = slot(zz, 1 - x, core)
                arrive(kind, which)
                push(kind, which, twin)

    for n in (2, 3):
        loads[n].wait()
    build(0, replica)
    relay_deep((0, 1))

    for k in range(1, replicas):
        build(k, (replica + k) % replicas)
    relay_side((0, 1))
    relay_deep((2,))

    for n in (4, 5, 6):
        loads[n].wait()
    wide_sum = upper_sum = None
    for zz in [z] + others:
        for kind in range(2):
            if zz is z:
                arrive(kind, twin)
            else:
                arrive(kind, slot(zz, x, 1 - core))
            arrive(kind, slot(zz, 1 - x, 1 - core))
        for n in range(4):
            base = n * share
            which = zz * 4 + n
            features[base : base + share, :count] = held_tok[which]
            features[base : base + split, count:] = held_nxt[which, :, :nexts]
            features[base + split : base + share, count:] = held_nxt[which, :, nexts:]
        turned = features[...].T
        at = pl.ds(pl.multiple_of(zz * group, 16), group)
        first, second = dot(turned, gate[at]), dot(turned, upper[at])
        wide_sum = first if wide_sum is None else wide_sum + first
        upper_sum = second if upper_sum is None else upper_sum + second
    mixed = (wide_sum / (1.0 + jnp.exp(-wide_sum)) * upper_sum).astype(KIND)
    relay_side((2,))
    tall = strip * TILE
    for n in range(rows // tall):
        hidden[n] = mixed[:count, n * tall : (n + 1) * tall]
    loads[8].wait()
    waved = dot(mixed, turn[...])
    rate = -STEP_RATE / replicas
    tops = waved[:count].astype(KIND).T
    tail = jnp.concatenate([mixed[count:], (waved[count:] * rate).astype(KIND)], axis=1)

    for n in (7, 9):
        loads[n].wait()
    tall = strip * TILE
    for n in range(rows // tall):
        low = n * tall // 2
        flat = slice(low, low + tall // 2)
        lower = slice(half + low, half + low + tall // 2)
        parts = []
        for start in range(0, breadth, chunk):
            span = slice(start, start + chunk)
            piece = momentum[n * tall : (n + 1) * tall, span]
            mixed = dot(row[...], jnp.concatenate([piece, piece], axis=0))
            parts.append(
                (
                    mixed[: tall // 2] * basis[0, flat, span].astype(jnp.float32)
                    + mixed[tall // 2 :] * basis[0, lower, span].astype(jnp.float32)
                ).astype(KIND)
            )
        early[flat] = dot(jnp.concatenate(parts, axis=1), gather[...])
    loads[10].wait()
    for zz in [z] + others:
        arrive(2, slot(zz, x, 1 - core))
        arrive(2, slot(zz, 1 - x, 1 - core))
    grads[...] = held_cot[...].reshape(breadth, count).T
    sums = early[...]
    for start in range(0, breadth, chunk):
        span = slice(start, start + chunk)
        lifted = dot(tops, grads[:, span])
        part = lifted[:half] * basis[0, :half, span].astype(jnp.float32) + lifted[
            half:
        ] * basis[0, half:, span].astype(jnp.float32)
        sums = sums + dot(part.astype(KIND), gather[span])
    values = sums.astype(KIND)
    mine[...] = sums.T[: mine.shape[0]].astype(KIND)

    def share_values(k):
        return pltpu.make_async_remote_copy(
            src_ref=mine,
            dst_ref=theirs.at[k - 1],
            send_sem=pass_send.at[k - 1],
            recv_sem=pass_recv.at[k - 1],
            device_id={"replica": (replica - k + replicas) % replicas},
            device_id_type=MESH,
        )

    for k in range(1, replicas):
        share_values(k).start()

    loads[11].wait()
    spans = [slice(start, start + wide) for start in range(0, breadth, wide)]
    for span in spans:
        spot = dot(values, spread[:, span])
        top = (spot * basis[0, :half, span].astype(jnp.float32)).astype(KIND)
        low = (spot * basis[0, half:, span].astype(jnp.float32)).astype(KIND)
        pair[0, :, span] = top
        pair[1, :, span] = low
        total[:, span] = dot(tail, jnp.concatenate([down[:, span], top, low], axis=0))
    for k in range(1, replicas):
        share_values(k).wait()
    blank = jnp.zeros((spread.shape[0] - mine.shape[0], half), jnp.float32)
    foreign = [
        jnp.concatenate([theirs[k].astype(jnp.float32), blank], axis=0).T.astype(KIND)
        for k in range(replicas - 1)
    ]

    quarter = nexts // 4
    short = nexts // size

    def fold_core(n):
        return pltpu.make_async_remote_copy(
            src_ref=stage_core.at[n], dst_ref=held_core.at[n],
            send_sem=fold_send.at[0, n], recv_sem=fold_recv.at[0, n],
            device_id={"tensor": twin}, device_id_type=MESH,
        )

    def fold_side(n):
        return pltpu.make_async_remote_copy(
            src_ref=stage_side.at[n], dst_ref=held_side.at[n],
            send_sem=fold_send.at[1, n], recv_sem=fold_recv.at[1, n],
            device_id={"tensor": side}, device_id_type=MESH,
        )

    def fold_deep(n, k):
        return pltpu.make_async_remote_copy(
            src_ref=stage_deep.at[n, others[k - 1]], dst_ref=held_deep.at[n, k - 1],
            send_sem=deep_send.at[n, k - 1], recv_sem=deep_recv.at[n, k - 1],
            device_id={"tensor": deep[k - 1]}, device_id_type=MESH,
        )

    def first_stage(n):
        span = spans[n]
        tops, lows = [], []
        for k in range(1, replicas):
            spot = dot(foreign[k - 1], spread[:, span])
            tops.append((spot * basis[k, :half, span].astype(jnp.float32)).astype(KIND))
            lows.append((spot * basis[k, half:, span].astype(jnp.float32)).astype(KIND))
        more = total[:, span]
        for top, low in zip(tops, lows):
            more = more + dot(tail[:, rows:], jnp.concatenate([top, low], axis=0))
        total[:, span] = more
        away = pl.ds(pl.multiple_of((1 - core) * 2 * quarter, 8), 2 * quarter)
        stage_core[n] = total[away, span].astype(KIND)
        fold_core(n).start()

    def second_stage(n):
        span = spans[n]
        fold_core(n).wait()
        base = core * 2 * quarter
        away = pl.ds(pl.multiple_of(base + (1 - x) * quarter, 8), quarter)
        here = pl.ds(pl.multiple_of(base + x * quarter, 8), quarter)
        got = pl.ds(pl.multiple_of((1 - x) * quarter, 8), quarter)
        left = pl.ds(pl.multiple_of(x * quarter, 8), quarter)
        stage_side[n] = (total[away, span] + held_core[n, got].astype(jnp.float32)).astype(KIND)
        fold_side(n).start()
        total[here, span] = total[here, span] + held_core[n, left].astype(jnp.float32)

    def third_stage(n):
        span = spans[n]
        fold_side(n).wait()
        base = core * 2 * quarter + x * quarter
        here = pl.ds(pl.multiple_of(base, 8), quarter)
        full = total[here, span] + held_side[n].astype(jnp.float32)
        for zz in range(depth):
            piece = full[zz * short : (zz + 1) * short]
            stage_deep[n, zz] = piece.astype(KIND)
            split_sum[n, zz] = piece
        for k in range(1, depth):
            fold_deep(n, k).start()

    steps = len(spans)
    lag, far = 2, 4
    for n in range(steps + far):
        if n < steps:
            first_stage(n)
        if 0 <= n - lag < steps:
            second_stage(n - lag)
        if 0 <= n - far:
            third_stage(n - far)
    for n in range(steps):
        span = spans[n]
        piece = split_sum[n, z]
        for k in range(1, depth):
            fold_deep(n, k).wait()
            piece = piece + held_deep[n, k - 1].astype(jnp.float32)
        out[:, span] = piece
    for copy in copies:
        copy.wait_send()


def step_pass(args, consts, size, replicas, strip, chunk, wide):
    tok, nxt, cot, gate, upper, down, momentum, indices = args
    share, count = tok.shape
    nexts = nxt.shape[0]
    rows, breadth = down.shape
    half = rows // 2
    depth = size // 4
    short = nexts // size
    columns = indices.shape[3]
    ribbon = columns + -columns % 128
    steps = breadth // wide
    quarter = nexts // 4
    pushes = 3 * (depth + 1 + 3 * depth - 2)

    def like(array):
        return pltpu.VMEM(array.shape, array.dtype)

    return pl.pallas_call(
        functools.partial(step_kernel, size, replicas, strip, chunk, wide),
        out_shape=(
            jax.ShapeDtypeStruct((short, breadth), jnp.float32),
            pltpu.VMEM((rows // (strip * TILE), count, strip * TILE), KIND),
            pltpu.VMEM((count, breadth), KIND),
            pltpu.VMEM((2, half, breadth), KIND),
            pltpu.VMEM((rows, breadth), KIND),
        ),
        in_specs=[ANY] * (len(args) + len(consts)),
        out_specs=(VMEM,) * 5,
        scratch_shapes=[
            like(nxt),
            pltpu.VMEM((size, share, count), KIND),
            pltpu.VMEM((size, share // 2, 2 * nexts), KIND),
            pltpu.VMEM((size, share, count), KIND),
            like(gate), like(upper), like(down), like(indices),
            pltpu.VMEM((ribbon, breadth), KIND),
            pltpu.VMEM((breadth, ribbon), KIND),
            *[like(const) for const in consts],
            pltpu.VMEM((4 * share, count + nexts), KIND),
            pltpu.VMEM((replicas, rows, breadth), KIND),
            pltpu.VMEM((half, ribbon), jnp.float32),
            pltpu.VMEM((columns, half), KIND),
            pltpu.VMEM((replicas - 1, columns, half), KIND),
            pltpu.VMEM((nexts, breadth), jnp.float32),
            pltpu.VMEM((steps, 2 * quarter, wide), KIND),
            pltpu.VMEM((steps, 2 * quarter, wide), KIND),
            pltpu.VMEM((steps, quarter, wide), KIND),
            pltpu.VMEM((steps, quarter, wide), KIND),
            pltpu.VMEM((steps, depth, short, wide), KIND),
            pltpu.VMEM((steps, depth - 1, short, wide), KIND),
            pltpu.VMEM((steps, depth, short, wide), jnp.float32),
            pltpu.SemaphoreType.DMA((pushes,)),
            pltpu.SemaphoreType.DMA((3, size)),
            pltpu.SemaphoreType.DMA((12,)),
            pltpu.SemaphoreType.DMA((replicas - 1,)),
            pltpu.SemaphoreType.DMA((replicas - 1,)),
            pltpu.SemaphoreType.DMA((2, steps)),
            pltpu.SemaphoreType.DMA((2, steps)),
            pltpu.SemaphoreType.DMA((steps, depth - 1)),
            pltpu.SemaphoreType.DMA((steps, depth - 1)),
        ],
        compiler_params=pltpu.CompilerParams(
            collective_id=0, has_side_effects=True, vmem_limit_bytes=44 * 2**20
        ),
        name="step_pass",
    )(*[pltpu.with_memory_space_constraint(array, pltpu.HBM) for array in [*args, *consts]])


def kept_kernel(tall, chunk, hidden, grads, momentum, pair, inverse, raw, kept, out):
    step = pl.program_id(0)
    breadth = grads.shape[1]
    low = pl.ds(pl.multiple_of(step * (tall // 2), 8), tall // 2)
    here = pl.ds(pl.multiple_of(step * tall, 8), tall)
    left = jnp.concatenate([hidden[step].T, inverse[...]], axis=1)
    for start in range(0, breadth, chunk):
        span = slice(start, start + chunk)
        right = jnp.concatenate([grads[:, span], pair[0, low, span], pair[1, low, span]], axis=0)
        kept[0, :, span] = (
            BETA_DECAY * momentum[here, span].astype(jnp.float32) + dot(left, right)
        ).astype(KIND)

    @pl.when(step == 0)
    def _():
        out[...] = raw[...].astype(KIND)


def whole_block(array):
    return pl.BlockSpec(array.shape, lambda i: (0,) * array.ndim)


def kept_pass(hidden, grads, momentum, pair, raw, strip, chunk):
    rows, breadth = momentum.shape
    tall = strip * TILE
    inverse = jnp.asarray(-halves(strip).T, jnp.float32).astype(KIND)
    return pl.pallas_call(
        functools.partial(kept_kernel, tall, chunk),
        grid=(rows // tall,),
        out_shape=(
            jax.ShapeDtypeStruct((1, rows, breadth), KIND),
            jax.ShapeDtypeStruct(raw.shape, KIND),
        ),
        in_specs=[VMEM, VMEM, VMEM, VMEM, whole_block(inverse), whole_block(raw)],
        out_specs=(
            pl.BlockSpec((1, tall, breadth), lambda i: (0, i, 0)),
            whole_block(raw),
        ),
        compiler_params=pltpu.CompilerParams(vmem_limit_bytes=24 * 2**20),
        name="kept_pass",
    )(hidden, grads, momentum, pair, inverse, raw)


def on_device(
    tokens, next_tokens, cotangent, gate_weight, up_weight, down_weight, momentum, indices
):
    size = lax.axis_size("tensor")
    replicas = lax.axis_size("replica")
    share = tokens.shape[1]
    nexts = next_tokens.shape[0]
    breadth = share * size
    tile_rows = indices.shape[1]
    strip = next(n for n in (2, 1) if tile_rows % n == 0)
    chunk = next(n for n in (256, 128) if breadth % n == 0)
    wide = 2 * chunk if breadth % (2 * chunk) == 0 else chunk

    high, low = split_bf16(BETA_DECAY * halves(strip))
    depth, short = size // 4, nexts // size
    order = np.zeros((nexts, nexts))
    for n in range(nexts):
        owner, rest = n // short, n % short
        z, x, core = owner // 4, (owner // 2) % 2, owner % 2
        order[n, ((core * 2 + x) * depth + z) * short + rest] = 1.0
    consts = [
        jnp.concatenate([high, low], axis=1),
        jnp.asarray(halves(tile_rows).T, jnp.float32).astype(KIND),
        jnp.asarray(np.kron(np.eye(chunk // TILE), cosine_table()), jnp.float32).astype(KIND),
        jnp.asarray(order, KIND),
    ]
    args = [
        tokens.T, next_tokens, cotangent.T, gate_weight, up_weight, down_weight, momentum,
        jnp.swapaxes(indices, 2, 3),
    ]
    raw, hidden, grads, pair, held = step_pass(args, consts, size, replicas, strip, chunk, wide)
    kept, output = kept_pass(hidden, grads, held, pair, raw, strip, chunk)
    return (output, kept)


def solution(mesh):
    return jax.shard_map(
        on_device,
        mesh=mesh,
        in_specs=(
            P("replica", "tensor"),
            P("replica", "tensor"),
            P("replica", "tensor"),
            P(None, "tensor"),
            P(None, "tensor"),
            P("tensor", None),
            P("replica", "tensor", None),
            P(None, "tensor", None, None),
        ),
        out_specs=(P(("replica", "tensor"), None), P("replica", "tensor", None)),
        check_vma=False,
    )
```

```python
import functools

import jax
import jax.numpy as jnp
import numpy as np
from jax import lax
from jax.experimental import pallas as pl
from jax.experimental.pallas import tpu as pltpu
from jax.sharding import PartitionSpec as P

TILE = 64
BETA_DECAY = 0.9
STEP_RATE = 0.1
MESH = pl.DeviceIdType.MESH
ANY = pl.BlockSpec(memory_space=pl.ANY)
VMEM = pl.BlockSpec(memory_space=pltpu.VMEM)
KIND = jnp.bfloat16


def cosine_table():
    freq = np.arange(TILE)[:, None]
    place = np.arange(TILE)[None, :]
    table = np.cos(np.pi * (2.0 * place + 1.0) * freq / (2.0 * TILE))
    return table * np.where(freq == 0, np.sqrt(1.0 / TILE), np.sqrt(2.0 / TILE))


def split_bf16(table):
    high = jnp.asarray(table, jnp.float32).astype(KIND)
    rest = jnp.asarray(table, jnp.float32) - high.astype(jnp.float32)
    return high, rest.astype(KIND)


def halves(count):
    table = cosine_table()
    eye = np.eye(count)
    return np.concatenate([np.kron(eye, table[0::2]), np.kron(eye, table[1::2])], axis=0)


def flip(index, bits):
    bit = 1
    while bit <= bits:
        if bits & bit:
            index = index + bit - 2 * bit * ((index // bit) % 2)
        bit *= 2
    return index


def dot(a, b):
    return jnp.dot(a, b, preferred_element_type=jnp.float32)


def contract(a, b, dim):
    return lax.dot_general(
        a, b, (((dim,), (dim,)), ((), ())), preferred_element_type=jnp.float32
    )


def strip_offsets(indices, which):
    tiles, keep, columns = indices.shape[1:]
    first = lax.broadcasted_iota(jnp.int32, (keep, columns), 0) * (TILE * TILE // keep)
    listed = [
        (indices[which, n] - first).astype(jnp.float32).astype(KIND) for n in range(tiles)
    ]
    return jnp.concatenate(listed, axis=0)


def step_kernel(
    size, replicas, strip, chunk, wide,
    tok, nxt, cot, gate_hbm, upper_hbm, down_hbm, momentum_hbm, indices_hbm,
    row_hbm, turn_hbm, across_hbm, order_hbm, inverse_hbm,
    out, momentum,
    nxt_in, held_tok, held_nxt, held_cot,
    gate, upper, down, indices, spread, gather, row, turn, across, order, inverse,
    features, basis, early, hidden, grads, pair, mine, theirs, total,
    stage_core, held_core, stage_side, held_side, stage_deep, held_deep, split_sum,
    send, recv, local, pass_send, pass_recv, fold_send, fold_recv, deep_send, deep_recv,
):
    depth = size // 4
    me = lax.axis_index("tensor")
    replica = lax.axis_index("replica")
    z, x, core = me // 4, (me // 2) % 2, me % 2
    share, count = tok.shape
    nexts = nxt.shape[0]
    rows, breadth = down.shape
    half = rows // 2
    split = share // 2
    group = 4 * share
    blocks, kept = (tok, held_nxt.at[me], cot), (held_tok, held_nxt, held_cot)

    def slot(zz, xx, cc):
        return (zz * 2 + xx) * 2 + cc

    names = [
        (nxt, nxt_in), (order_hbm, order), (indices_hbm, indices), (across_hbm, across),
        (tok, held_tok.at[me]), (gate_hbm, gate), (upper_hbm, upper), (row_hbm, row),
        (turn_hbm, turn), (momentum_hbm.at[0], momentum), (cot, held_cot.at[me]), (down_hbm, down),
        (inverse_hbm, inverse),
    ]
    loads = [
        pltpu.make_async_copy(source, target, local.at[n])
        for n, (source, target) in enumerate(names)
    ]
    for load in loads:
        load.start()

    others = [flip(z, k) for k in range(1, depth)]
    deep = [slot(zz, x, core) for zz in others]
    side, twin = slot(z, 1 - x, core), slot(z, x, 1 - core)
    barrier = pltpu.get_barrier_semaphore()
    for target in deep + [side, twin]:
        pl.semaphore_signal(barrier, inc=1, device_id={"tensor": target}, device_id_type=MESH)
    for k in range(1, replicas):
        pl.semaphore_signal(
            barrier, inc=1, device_id={"replica": (replica + k) % replicas}, device_id_type=MESH
        )
    ribbon = spread.shape
    spread[...] = jnp.where(
        lax.broadcasted_iota(jnp.int32, ribbon, 1) // TILE
        == lax.broadcasted_iota(jnp.int32, ribbon, 0),
        1.0,
        0.0,
    ).astype(KIND)
    gather[...] = spread[...].T
    pl.semaphore_wait(barrier, depth + replicas)

    copies = []

    def push(kind, which, target, source=None):
        copy = pltpu.make_async_remote_copy(
            src_ref=kept[kind].at[which] if source is None else source,
            dst_ref=kept[kind].at[which],
            send_sem=send.at[len(copies)],
            recv_sem=recv.at[kind, which],
            device_id={"tensor": target},
            device_id_type=MESH,
        )
        copy.start()
        copies.append(copy)

    def arrive(kind, which):
        pltpu.make_async_remote_copy(
            src_ref=blocks[kind],
            dst_ref=kept[kind].at[which],
            send_sem=send.at[0],
            recv_sem=recv.at[kind, which],
            device_id={"tensor": twin},
            device_id_type=MESH,
        ).wait_recv()

    for target in deep + [side, twin]:
        push(0, me, target, tok)
    loads[0].wait()
    loads[1].wait()
    turned = contract(nxt_in[...], order[...], 0)
    held_nxt[me] = jnp.concatenate([turned[:split], turned[split:]], axis=1).astype(KIND)
    for target in deep + [side, twin]:
        push(1, me, target)
    for target in deep:
        push(2, me, target, cot)

    place = (lax.broadcasted_iota(jnp.int32, (half, chunk), 1) % TILE).astype(jnp.float32)

    def build(slab, offsets, span):
        where = dot(offsets, spread[: offsets.shape[1], span])
        odd = where >= TILE
        hot = jnp.where(jnp.where(odd, where - TILE, where) == place, 1.0, 0.0)
        waves = dot(hot.astype(KIND), across[...])
        basis[slab, :half, span] = jnp.where(odd, 0.0, waves).astype(KIND)
        basis[slab, half:, span] = jnp.where(odd, waves, 0.0).astype(KIND)

    def from_deep(kind, which):
        arrive(kind, which)
        push(kind, which, side)
        push(kind, which, twin)

    def from_side(kind, zz):
        which = slot(zz, 1 - x, core)
        arrive(kind, which)
        push(kind, which, twin)

    def send_late():
        for target in (side, twin):
            push(2, me, target, cot)

    def drain(events, most):
        for _ in range(min(most, len(events))):
            events.pop(0)()

    bind = functools.partial
    first_events = []
    for kind in range(2):
        first_events.append(bind(from_side, kind, z))
        first_events += [bind(from_deep, kind, which) for which in deep]
    first_events.append(send_late)
    for kind in range(2):
        first_events += [bind(from_side, kind, zz) for zz in others]
    last_events = [bind(from_deep, 2, which) for which in deep]
    last_events += [bind(from_side, 2, zz) for zz in [z] + others]

    narrow = [slice(start, start + chunk) for start in range(0, breadth, chunk)]
    tall = strip * TILE

    def spectrum(n):
        low = n * tall // 2
        flat = slice(low, low + tall // 2)
        lower = slice(half + low, half + low + tall // 2)
        parts = []
        for span in narrow:
            piece = momentum[n * tall : (n + 1) * tall, span]
            mixed = dot(row[...], jnp.concatenate([piece, piece], axis=0))
            parts.append(
                (
                    mixed[: tall // 2] * basis[0, flat, span].astype(jnp.float32)
                    + mixed[tall // 2 :] * basis[0, lower, span].astype(jnp.float32)
                ).astype(KIND)
            )
        early[flat] = dot(jnp.concatenate(parts, axis=1), gather[...])

    for n in (2, 3):
        loads[n].wait()
    offsets = strip_offsets(indices, replica)
    for span in narrow:
        build(0, offsets, span)
    for k in range(1, replicas):
        offsets = strip_offsets(indices, (replica + k) % replicas)
        for span in narrow:
            build(k, offsets, span)
            drain(first_events, 1)
    for n in (7, 9):
        loads[n].wait()
    strips = list(range(rows // tall))
    while first_events:
        if len(strips) > 4:
            spectrum(strips.pop(0))
        drain(first_events, 2)

    for n in (4, 5, 6):
        loads[n].wait()
    wide_sum = upper_sum = None
    for zz in [z] + others:
        for kind in range(2):
            if zz is z:
                arrive(kind, twin)
            else:
                arrive(kind, slot(zz, x, 1 - core))
            arrive(kind, slot(zz, 1 - x, 1 - core))
        for n in range(4):
            base = n * share
            which = zz * 4 + n
            features[base : base + share, :count] = held_tok[which]
            features[base : base + split, count:] = held_nxt[which, :, :nexts]
            features[base + split : base + share, count:] = held_nxt[which, :, nexts:]
        turned = features[...].T
        at = pl.ds(pl.multiple_of(zz * group, 16), group)
        first, second = dot(turned, gate[at]), dot(turned, upper[at])
        wide_sum = first if wide_sum is None else wide_sum + first
        upper_sum = second if upper_sum is None else upper_sum + second
        drain(last_events, 1)
    mixed = (wide_sum / (1.0 + jnp.exp(-wide_sum)) * upper_sum).astype(KIND)
    drain(last_events, 1)
    for n in range(rows // tall):
        hidden[n] = mixed[:count, n * tall : (n + 1) * tall]
    loads[8].wait()
    waved = dot(mixed, turn[...])
    rate = -STEP_RATE / replicas
    tops = waved[:count].astype(KIND).T
    tail = jnp.concatenate([mixed[count:], (waved[count:] * rate).astype(KIND)], axis=1)

    while strips or last_events:
        if strips:
            spectrum(strips.pop(0))
        drain(last_events, 1)
    loads[10].wait()
    for zz in [z] + others:
        arrive(2, slot(zz, x, 1 - core))
        arrive(2, slot(zz, 1 - x, 1 - core))
    grads[...] = held_cot[...].reshape(breadth, count).T
    sums = early[...]
    for start in range(0, breadth, chunk):
        span = slice(start, start + chunk)
        lifted = dot(tops, grads[:, span])
        part = lifted[:half] * basis[0, :half, span].astype(jnp.float32) + lifted[
            half:
        ] * basis[0, half:, span].astype(jnp.float32)
        sums = sums + dot(part.astype(KIND), gather[span])
    values = sums.astype(KIND)
    mine[...] = sums.T[: mine.shape[0]].astype(KIND)

    def share_values(k):
        return pltpu.make_async_remote_copy(
            src_ref=mine,
            dst_ref=theirs.at[k - 1],
            send_sem=pass_send.at[k - 1],
            recv_sem=pass_recv.at[k - 1],
            device_id={"replica": (replica - k + replicas) % replicas},
            device_id_type=MESH,
        )

    for k in range(1, replicas):
        share_values(k).start()

    loads[11].wait()
    spans = [slice(start, start + wide) for start in range(0, breadth, wide)]
    for span in spans:
        spot = dot(values, spread[:, span])
        top = (spot * basis[0, :half, span].astype(jnp.float32)).astype(KIND)
        low = (spot * basis[0, half:, span].astype(jnp.float32)).astype(KIND)
        pair[0, :, span] = top
        pair[1, :, span] = low
        total[:, span] = dot(tail, jnp.concatenate([down[:, span], top, low], axis=0))
    for k in range(1, replicas):
        share_values(k).wait()
    blank = jnp.zeros((spread.shape[0] - mine.shape[0], half), jnp.float32)
    foreign = [
        jnp.concatenate([theirs[k].astype(jnp.float32), blank], axis=0).T.astype(KIND)
        for k in range(replicas - 1)
    ]

    quarter = nexts // 4
    short = nexts // size

    def fold_core(n):
        return pltpu.make_async_remote_copy(
            src_ref=stage_core.at[n], dst_ref=held_core.at[n],
            send_sem=fold_send.at[0, n], recv_sem=fold_recv.at[0, n],
            device_id={"tensor": twin}, device_id_type=MESH,
        )

    def fold_side(n):
        return pltpu.make_async_remote_copy(
            src_ref=stage_side.at[n], dst_ref=held_side.at[n],
            send_sem=fold_send.at[1, n], recv_sem=fold_recv.at[1, n],
            device_id={"tensor": side}, device_id_type=MESH,
        )

    def fold_deep(n, k):
        return pltpu.make_async_remote_copy(
            src_ref=stage_deep.at[n, others[k - 1]], dst_ref=held_deep.at[n, k - 1],
            send_sem=deep_send.at[n, k - 1], recv_sem=deep_recv.at[n, k - 1],
            device_id={"tensor": deep[k - 1]}, device_id_type=MESH,
        )

    def first_stage(n):
        span = spans[n]
        tops, lows = [], []
        for k in range(1, replicas):
            spot = dot(foreign[k - 1], spread[:, span])
            tops.append((spot * basis[k, :half, span].astype(jnp.float32)).astype(KIND))
            lows.append((spot * basis[k, half:, span].astype(jnp.float32)).astype(KIND))
        more = total[:, span]
        for top, low in zip(tops, lows):
            more = more + dot(tail[:, rows:], jnp.concatenate([top, low], axis=0))
        total[:, span] = more
        away = pl.ds(pl.multiple_of((1 - core) * 2 * quarter, 8), 2 * quarter)
        stage_core[n] = total[away, span].astype(KIND)
        fold_core(n).start()

    def second_stage(n):
        span = spans[n]
        fold_core(n).wait()
        base = core * 2 * quarter
        away = pl.ds(pl.multiple_of(base + (1 - x) * quarter, 8), quarter)
        here = pl.ds(pl.multiple_of(base + x * quarter, 8), quarter)
        got = pl.ds(pl.multiple_of((1 - x) * quarter, 8), quarter)
        left = pl.ds(pl.multiple_of(x * quarter, 8), quarter)
        stage_side[n] = (total[away, span] + held_core[n, got].astype(jnp.float32)).astype(KIND)
        fold_side(n).start()
        total[here, span] = total[here, span] + held_core[n, left].astype(jnp.float32)

    def third_stage(n):
        span = spans[n]
        fold_side(n).wait()
        base = core * 2 * quarter + x * quarter
        here = pl.ds(pl.multiple_of(base, 8), quarter)
        full = total[here, span] + held_side[n].astype(jnp.float32)
        for zz in range(depth):
            piece = full[zz * short : (zz + 1) * short]
            stage_deep[n, zz] = piece.astype(KIND)
            split_sum[n, zz] = piece
        for k in range(1, depth):
            fold_deep(n, k).start()

    def remain(n):
        rows_here = slice(n * tall, (n + 1) * tall)
        low = slice(n * tall // 2, (n + 1) * tall // 2)
        left = jnp.concatenate([hidden[n].T, inverse[...]], axis=1)
        for span in narrow:
            right = jnp.concatenate([grads[:, span], pair[0, low, span], pair[1, low, span]], axis=0)
            momentum[rows_here, span] = (
                BETA_DECAY * momentum[rows_here, span].astype(jnp.float32) + dot(left, right)
            ).astype(KIND)

    loads[12].wait()
    strips = list(range(rows // tall))
    steps = len(spans)
    lag, far = 2, 4
    for n in range(steps + far):
        if n < steps:
            first_stage(n)
        if 0 <= n - lag < steps:
            second_stage(n - lag)
        if 0 <= n - far:
            third_stage(n - far)
        if n >= steps:
            for _ in range(1 if n == steps else 2):
                if strips:
                    remain(strips.pop(0))
    while strips:
        remain(strips.pop(0))
    for n in range(steps):
        span = spans[n]
        piece = split_sum[n, z]
        for k in range(1, depth):
            fold_deep(n, k).wait()
            piece = piece + held_deep[n, k - 1].astype(jnp.float32)
        out[:, span] = piece
    for copy in copies:
        copy.wait_send()


def step_pass(args, consts, size, replicas, strip, chunk, wide):
    tok, nxt, cot, gate, upper, down, momentum, indices = args
    share, count = tok.shape
    nexts = nxt.shape[0]
    rows, breadth = down.shape
    half = rows // 2
    depth = size // 4
    short = nexts // size
    columns = indices.shape[3]
    ribbon = columns + -columns % 128
    steps = breadth // wide
    quarter = nexts // 4
    pushes = 3 * (depth + 1 + 3 * depth - 2)

    def like(array):
        return pltpu.VMEM(array.shape, array.dtype)

    return pl.pallas_call(
        functools.partial(step_kernel, size, replicas, strip, chunk, wide),
        out_shape=(
            pltpu.VMEM((short, breadth), jnp.float32),
            pltpu.VMEM((rows, breadth), KIND),
        ),
        in_specs=[ANY] * (len(args) + len(consts)),
        out_specs=(VMEM,) * 2,
        scratch_shapes=[
            like(nxt),
            pltpu.VMEM((size, share, count), KIND),
            pltpu.VMEM((size, share // 2, 2 * nexts), KIND),
            pltpu.VMEM((size, share, count), KIND),
            like(gate), like(upper), like(down), like(indices),
            pltpu.VMEM((ribbon, breadth), KIND),
            pltpu.VMEM((breadth, ribbon), KIND),
            *[like(const) for const in consts],
            pltpu.VMEM((4 * share, count + nexts), KIND),
            pltpu.VMEM((replicas, rows, breadth), KIND),
            pltpu.VMEM((half, ribbon), jnp.float32),
            pltpu.VMEM((rows // (strip * TILE), count, strip * TILE), KIND),
            pltpu.VMEM((count, breadth), KIND),
            pltpu.VMEM((2, half, breadth), KIND),
            pltpu.VMEM((columns, half), KIND),
            pltpu.VMEM((replicas - 1, columns, half), KIND),
            pltpu.VMEM((nexts, breadth), jnp.float32),
            pltpu.VMEM((steps, 2 * quarter, wide), KIND),
            pltpu.VMEM((steps, 2 * quarter, wide), KIND),
            pltpu.VMEM((steps, quarter, wide), KIND),
            pltpu.VMEM((steps, quarter, wide), KIND),
            pltpu.VMEM((steps, depth, short, wide), KIND),
            pltpu.VMEM((steps, depth - 1, short, wide), KIND),
            pltpu.VMEM((steps, depth, short, wide), jnp.float32),
            pltpu.SemaphoreType.DMA((pushes,)),
            pltpu.SemaphoreType.DMA((3, size)),
            pltpu.SemaphoreType.DMA((13,)),
            pltpu.SemaphoreType.DMA((replicas - 1,)),
            pltpu.SemaphoreType.DMA((replicas - 1,)),
            pltpu.SemaphoreType.DMA((2, steps)),
            pltpu.SemaphoreType.DMA((2, steps)),
            pltpu.SemaphoreType.DMA((steps, depth - 1)),
            pltpu.SemaphoreType.DMA((steps, depth - 1)),
        ],
        compiler_params=pltpu.CompilerParams(
            collective_id=0, has_side_effects=True, vmem_limit_bytes=52 * 2**20
        ),
        name="step_pass",
    )(*[pltpu.with_memory_space_constraint(array, pltpu.HBM) for array in [*args, *consts]])


def leave_kernel(parts, ready, raw, kept, out, sems):
    tall = ready.shape[0] // parts
    copies = [
        pltpu.make_async_copy(
            ready.at[n * tall : (n + 1) * tall], kept.at[0, n * tall : (n + 1) * tall], sems.at[n]
        )
        for n in range(parts)
    ]
    for copy in copies:
        copy.start()
    out[...] = raw[...].astype(KIND)
    for copy in copies:
        copy.wait()


def leave_pass(ready, raw, parts):
    return pl.pallas_call(
        functools.partial(leave_kernel, parts),
        out_shape=(
            jax.ShapeDtypeStruct((1,) + ready.shape, KIND),
            jax.ShapeDtypeStruct(raw.shape, KIND),
        ),
        in_specs=[VMEM, VMEM],
        out_specs=(ANY, VMEM),
        scratch_shapes=[pltpu.SemaphoreType.DMA((parts,))],
        compiler_params=pltpu.CompilerParams(vmem_limit_bytes=8 * 2**20),
        name="leave_pass",
    )(ready, raw)


def on_device(
    tokens, next_tokens, cotangent, gate_weight, up_weight, down_weight, momentum, indices
):
    size = lax.axis_size("tensor")
    replicas = lax.axis_size("replica")
    share = tokens.shape[1]
    nexts = next_tokens.shape[0]
    breadth = share * size
    tile_rows = indices.shape[1]
    strip = next(n for n in (2, 1) if tile_rows % n == 0)
    chunk = next(n for n in (256, 128) if breadth % n == 0)
    wide = 2 * chunk if breadth % (2 * chunk) == 0 else chunk

    high, low = split_bf16(BETA_DECAY * halves(strip))
    depth, short = size // 4, nexts // size
    order = np.zeros((nexts, nexts))
    for n in range(nexts):
        owner, rest = n // short, n % short
        z, x, core = owner // 4, (owner // 2) % 2, owner % 2
        order[n, ((core * 2 + x) * depth + z) * short + rest] = 1.0
    consts = [
        jnp.concatenate([high, low], axis=1),
        jnp.asarray(halves(tile_rows).T, jnp.float32).astype(KIND),
        jnp.asarray(np.kron(np.eye(chunk // TILE), cosine_table()), jnp.float32).astype(KIND),
        jnp.asarray(order, KIND),
        jnp.asarray(-halves(strip).T, jnp.float32).astype(KIND),
    ]
    args = [
        tokens.T, next_tokens, cotangent.T, gate_weight, up_weight, down_weight, momentum,
        jnp.swapaxes(indices, 2, 3),
    ]
    raw, ready = step_pass(args, consts, size, replicas, strip, chunk, wide)
    kept, output = leave_pass(ready, raw, 7)
    return (output, kept)


def solution(mesh):
    return jax.shard_map(
        on_device,
        mesh=mesh,
        in_specs=(
            P("replica", "tensor"),
            P("replica", "tensor"),
            P("replica", "tensor"),
            P(None, "tensor"),
            P(None, "tensor"),
            P("tensor", None),
            P("replica", "tensor", None),
            P(None, "tensor", None, None),
        ),
        out_specs=(P(("replica", "tensor"), None), P("replica", "tensor", None)),
        check_vma=False,
    )
```
